32 devices in a mesh: rows: 8 (over z, core), pairs: 4 (over y, x).
Axes of the slice: x: 2, y: 2, z: 4, core: 2. Of those that a mesh axis runs over, the one named last changes fastest.
Arguments:
- observed: float32 [12288, 2048], P('rows', 'pairs'), as said below
- estimate: float32 [12288, 2048], P('rows', 'pairs'), may hold values from -0.054126587 to 0.054126587
- mask: int32 [12288, 2048], P('rows', 'pairs'), may hold values from 0 to 1
- threshold: float32 [2048], P('pairs'), may hold values from 0.02 to 0.12
Outputs:
- regrouped: float32 [2048, 12288], P(('rows', 'pairs'))
The draws below stay inside these ranges and needn't reach their ends.
Inputs may be any that keep to these rules, and one draw needn't show every extreme that they name: observed has entries of order 12288^-1/2.
All inputs are finite; a program needn't handle non-finite values.
Results may differ from the reference program's by a relative error of at most 0.0003.
Values sent between devices are 32-bit elements; how exact they have to be, the bound alone decides.
A program may use at most 128 MiB of HBM per device.

```python
import jax
import jax.numpy as jnp
from jax import lax

BW = 128
ROUNDS = 4
NS_STEPS = 3
ROWS = 12288
COLS = 2048
N_PAIRS = 4


def draw_observed(key, part):
    key_noise = jax.random.fold_in(key, 11)
    key_shared = jax.random.fold_in(key, 12)
    key_scale = jax.random.fold_in(key, 13)
    groups = COLS // (2 * BW)
    noise = jax.random.normal(key_noise, (ROWS, COLS), jnp.float32)
    shared = jax.random.normal(key_shared, (ROWS, groups, 1, BW), jnp.float32)
    colscale = jax.random.uniform(key_scale, (COLS,), jnp.float32, 0.6, 1.6)
    shared = jnp.broadcast_to(shared, (ROWS, groups, 2, BW)).reshape(ROWS, COLS)
    values = (noise + 0.7 * shared) * colscale[None, :] / jnp.sqrt(1.49 * ROWS)
    return values.astype(jnp.float32)


def touch_ends(array, rng, low, high):
    shape = array.shape
    place = [jax.random.randint(jax.random.fold_in(rng, axis), (), 0, shape[axis]) for axis in range(len(shape))]
    array = array.at[tuple(place)].set(low)
    longest = shape.index(max(shape))
    place[longest] = (place[longest] + 1) % shape[longest]
    return array.at[tuple(place)].set(high)


def block_levels(key, shape, shards, least, top_value):
    level = 1.0
    for dim, blocks in shards:
        steps = jax.random.uniform(jax.random.fold_in(jax.random.fold_in(key, 6), dim), (blocks,), jnp.float32, least / len(shards), top_value / len(shards))
        level = level * jnp.repeat(jnp.exp(steps), shape[dim] // blocks).reshape((-1,) + (1,) * (len(shape) - 1 - dim))
    return level


def centred(stream_key, extent, scale, limit, split=(), kind=jnp.bfloat16):
    drawn = scale * jax.random.normal(stream_key, extent, jnp.float32)
    if split:
        drawn = drawn * block_levels(stream_key, extent, split, -0.22, 0.18)
    return jnp.clip(drawn, -limit, limit).astype(kind)


def setup_inputs(seed: int = 0) -> dict:
    key_list = jax.random.split(jax.random.key(seed), 5)
    observed = draw_observed(jax.random.fold_in(key_list[4], 71), 0)
    estimate = centred(key_list[1], (ROWS, COLS), (ROWS ** -0.5), 0.054126587, ((0, 8), (1, 4)), jnp.float32)
    mask = touch_ends(jax.random.randint(key_list[2], (ROWS, COLS), 0, 2), jax.random.fold_in(key_list[2], 1), 0, 1).astype(jnp.int32)
    threshold = jnp.clip(0.02 + 0.09999999776482582 * jax.random.uniform(key_list[3], (COLS,), jnp.float32) ** block_levels(key_list[3], (COLS,), ((0, 4),), -0.2, 0.2), 0.02, 0.12)
    return {"observed": observed, "estimate": estimate, "mask": mask, "threshold": threshold}


HI = lax.Precision.HIGHEST

def whitening_of(gram):
    width = gram.shape[-1]
    eye = jnp.eye(width, dtype=jnp.float32)
    dsum = jnp.diagonal(gram, axis1=-2, axis2=-1) + 1e-06
    inv_root = 1.0 / jnp.sqrt(dsum)
    normed = gram * inv_root[..., :, None] * inv_root[..., None, :]
    fro = jnp.sqrt(lax.optimization_barrier(jnp.sum(normed * normed, axis=(-2, -1))))
    ymat = normed / fro[..., None, None]
    zmat = jnp.broadcast_to(eye, normed.shape)
    for step in range(NS_STEPS):
        tmat = 1.5 * eye - 0.5 * jnp.einsum('...ij,...jk->...ik', zmat, ymat, precision=HI)
        ymat = jnp.einsum('...ij,...jk->...ik', ymat, tmat, precision=HI)
        zmat = jnp.einsum('...ij,...jk->...ik', tmat, zmat, precision=HI)
    return inv_root[..., :, None] * zmat * jnp.sqrt(dsum)[..., None, :] / jnp.sqrt(fro)[..., None, None]

def reference(observed, estimate, mask, threshold):
    filled = jnp.where(mask == 1, observed, estimate)
    total = filled.shape[0]
    groups = N_PAIRS
    blocks = filled.reshape(total, groups, 4, BW)
    for round_index in range(ROUNDS):
        pairs = blocks.reshape(total, groups, 2, 2 * BW)
        gram = jnp.einsum('rdpi,rdpj->dpij', pairs, pairs, precision=HI)
        whitening = whitening_of(gram)
        pairs = jnp.einsum('rdpi,dpij->rdpj', pairs, whitening, precision=HI)
        blocks = pairs.reshape(total, groups, 4, BW)
        if round_index + 1 < ROUNDS:
            first = blocks[:, :, 1]
            third = blocks[:, :, 3]
            blocks = jnp.stack([blocks[:, :, 0], jnp.roll(third, 1, axis=1), blocks[:, :, 2], first], axis=2)
    filled = blocks.reshape(total, groups * 4 * BW)
    col_norm = jnp.sqrt(lax.optimization_barrier(jnp.sum(filled * filled, axis=0)) + 1e-06)
    factor = jnp.maximum(col_norm - threshold, 0.0) / col_norm
    shrunk = filled * factor[None, :]
    return shrunk.reshape(total, groups, 4 * BW).transpose(2, 1, 0).reshape(groups * 4 * BW, total)
```

```python
import functools

import jax
import jax.numpy as jnp
from jax import lax
from jax.experimental import pallas as pl
from jax.experimental.pallas import tpu as pltpu
from jax.sharding import PartitionSpec as P

MESH = pl.DeviceIdType.MESH
F32 = jnp.float32
BF16 = jnp.bfloat16
NN = (((1,), (0,)), ((), ()))
NT = (((1,), (1,)), ((), ()))


def split(a):
    high = a.astype(BF16)
    return high, (a - high.astype(F32)).astype(BF16)


def dot_parts(a, b, dims):
    def one(x, y):
        return lax.dot_general(x, y, dims, preferred_element_type=F32)

    return one(a[0], b[0]) + (one(a[0], b[1]) + one(a[1], b[0]))


def dot3(a, b, dims=NN):
    return dot_parts(split(a), split(b), dims)


def whitening_t(gram):
    width = gram.shape[0]
    eye = (
        lax.broadcasted_iota(jnp.int32, (width, width), 0)
        == lax.broadcasted_iota(jnp.int32, (width, width), 1)
    ).astype(F32)
    on_diag = gram * eye
    d_col = jnp.sum(on_diag, axis=1, keepdims=True) + 1e-06
    d_row = jnp.sum(on_diag, axis=0, keepdims=True) + 1e-06
    i_col = 1.0 / jnp.sqrt(d_col)
    i_row = 1.0 / jnp.sqrt(d_row)
    normed = gram * i_col * i_row
    sq = jnp.sum(jnp.sum(normed * normed, axis=1, keepdims=True), axis=0, keepdims=True)
    fro = jnp.sqrt(sq)
    y = normed / fro
    t = 1.5 * eye - 0.5 * y
    z = t
    y = dot3(y, t)
    t = 1.5 * eye - 0.5 * dot3(z, y)
    y, z = dot3(y, t), dot3(t, z)
    t = 1.5 * eye - 0.5 * dot3(z, y)
    z = dot3(t, z)
    return jnp.sqrt(d_col) * z * i_row / jnp.sqrt(fro)


def join(ss, sm, mm):
    top = jnp.concatenate([ss, sm], axis=1)
    low = jnp.concatenate([sm.T, mm], axis=1)
    return jnp.concatenate([top, low], axis=0)


def kernel(
    n_rows, n_pairs, step,
    obs_ref, est_ref, mask_ref, thr_ref, out_ref,
    x, perm, pay, land, res, gmm_out, gmm_in, v_buf, send,
    rs_s, rs_r, ag_s, ag_r, pm_s, pm_r, pg_s, pg_r, out_s, out_r, own_sem,
):
    me = lax.axis_index("rows")
    group = lax.axis_index("pairs")
    n = n_rows * n_pairs
    bw = x.shape[2]
    rows = x.shape[3]
    chunks = rows // step
    each = send.shape[1]

    barrier = pltpu.get_barrier_semaphore()
    my_k = me * n_pairs + group

    def greet(i, carry):
        k = lax.rem(my_k + i, n)
        pl.semaphore_signal(
            barrier, inc=1, device_id=(k // n_pairs, lax.rem(k, n_pairs)), device_id_type=MESH
        )
        return carry

    lax.fori_loop(1, n, greet, 0)

    for slot in range(4):
        cols = slice(slot * bw, (slot + 1) * bw)
        for c in range(chunks):
            part = slice(c * step, (c + 1) * step)
            filled = jnp.where(mask_ref[part, cols] == 1, obs_ref[part, cols], est_ref[part, cols])
            x[0, slot, :, part] = filled.T

    def cols_of(c):
        return pl.ds(pl.multiple_of(c * step, step), step)

    def full_gram(s, m):
        total = jnp.zeros((2 * bw, 2 * bw), F32)
        for c in range(chunks):
            part = slice(c * step, (c + 1) * step)
            both = split(jnp.concatenate([s[:, part], m[:, part]], axis=0))
            total += dot_parts(both, both, NT)
        return total

    def cross_gram(s, m):
        total = jnp.zeros((bw, bw), F32)
        for c in range(chunks):
            part = slice(c * step, (c + 1) * step)
            total += dot_parts(split(s[:, part]), split(m[:, part]), NT)
        return total

    def all_reduce(b, blocks):
        count = len(blocks)
        piece = count * bw // n_rows
        base = sum(COUNTS[:b]) * bw
        lbase = base // n_rows
        for i, block in enumerate(blocks):
            pay[base + i * bw : base + (i + 1) * bw, :] = block
        if b == 0:
            pl.semaphore_wait(barrier, n - 1)

        def area(ref, p):
            return ref.at[pl.ds(pl.multiple_of(base + p * piece, 8), piece)]

        def scatter(off, carry):
            peer = lax.rem(me + off, n_rows)
            pltpu.make_async_remote_copy(
                area(pay, peer), land.at[off, pl.ds(lbase, piece)],
                rs_s.at[b], rs_r.at[b], device_id=(peer, group), device_id_type=MESH,
            ).start()
            return carry

        lax.fori_loop(1, n_rows, scatter, 0)
        others = land.at[pl.ds(1, n_rows - 1), pl.ds(lbase, piece)]
        pltpu.make_async_copy(others, others, rs_r.at[b]).wait()
        mine = pl.ds(pl.multiple_of(base + me * piece, 8), piece)
        total = pay[mine, :]
        for off in range(1, n_rows):
            total += land[off, lbase : lbase + piece, :]
        res[mine, :] = total

        def gather(off, carry):
            peer = lax.rem(me + off, n_rows)
            pltpu.make_async_remote_copy(
                area(res, me), area(res, me),
                ag_s.at[b], ag_r.at[b], device_id=(peer, group), device_id_type=MESH,
            ).start()
            return carry

        lax.fori_loop(1, n_rows, gather, 0)
        pltpu.make_async_copy(others, others, ag_r.at[b]).wait()
        return [res[base + i * bw : base + (i + 1) * bw, :] for i in range(count)]

    def settle(b):
        piece = COUNTS[b] * bw // n_rows
        lbase = sum(COUNTS[:b]) * bw // n_rows
        others = land.at[pl.ds(1, n_rows - 1), pl.ds(lbase, piece)]
        pltpu.make_async_copy(others, others, rs_s.at[b]).wait()
        pltpu.make_async_copy(others, others, ag_s.at[b]).wait()

    def put(v_half, s, m, write):
        v_parts = split(v_half)
        for c in range(chunks):
            part = slice(c * step, (c + 1) * step)
            both = split(jnp.concatenate([s[:, part], m[:, part]], axis=0))
            write(part, dot_parts(v_parts, both, NN))

    def into(ref):
        def write(part, value):
            ref[:, part] = value
        return write

    def pass_on(i, block, gmm):
        gmm_out[i] = gmm
        right = lax.rem(group + 1, n_pairs)
        data = pltpu.make_async_remote_copy(
            block, perm.at[i], pm_s.at[i], pm_r.at[i],
            device_id=(me, right), device_id_type=MESH,
        )
        data.start()
        small = pltpu.make_async_remote_copy(
            gmm_out.at[i], gmm_in.at[i], pg_s.at[i], pg_r.at[i],
            device_id=(me, right), device_id_type=MESH,
        )
        small.start()
        return data, small

    def new_grams(v, gram):
        vg = dot3(v, gram)
        return dot3(vg[:bw], v[:bw], NT), dot3(vg[bw:], v[bw:], NT)

    def deliver(half):
        count = n // 2

        def go(i, carry):
            k = half * count + lax.rem(my_k + i, count)

            @pl.when(k != my_k)
            def _():
                pltpu.make_async_remote_copy(
                    send.at[k], out_ref.at[my_k], out_s, out_r,
                    device_id=(k // n_pairs, lax.rem(k, n_pairs)), device_id_type=MESH,
                ).start()

            @pl.when(k == my_k)
            def _():
                pltpu.make_async_copy(send.at[k], out_ref.at[my_k], own_sem).start()

            return carry

        lax.fori_loop(0, count, go, 0)

    def finish(half, v, gram, s, m):
        vg = dot3(v, gram)
        squares = jnp.sum(vg * v, axis=1, keepdims=True)
        norm = jnp.sqrt(squares + 1e-06)
        level = thr_ref[2 * half * bw : 2 * (half + 1) * bw, :]
        scaled = (jnp.maximum(norm - level, 0.0) / norm) * v
        per_block = bw // each
        for j in range(2):
            def write(part, value):
                for i in range(per_block):
                    send[(2 * half + j) * per_block + i, :, part] = value[i * each : (i + 1) * each]
            put(scaled[j * bw : (j + 1) * bw], s, m, write)
        deliver(half)

    ga = full_gram(x.at[0, 0], x.at[0, 1])
    gb = full_gram(x.at[0, 2], x.at[0, 3])
    blocks = []
    for g in (ga, gb):
        blocks += [g[:bw, :bw], g[:bw, bw:], g[bw:, bw:]]
    got = all_reduce(0, blocks)
    gb = join(*got[3:])
    vb = whitening_t(gb)
    put(vb[bw:], x.at[0, 2], x.at[0, 3], into(x.at[1, 3]))
    bs, bm = new_grams(vb, gb)
    sent = [pass_on(0, x.at[1, 3], bm)]
    ga = join(*got[:3])
    va = whitening_t(ga)
    put(va[bw:], x.at[0, 0], x.at[0, 1], into(x.at[1, 1]))
    put(vb[:bw], x.at[0, 2], x.at[0, 3], into(x.at[1, 2]))
    as_, am = new_grams(va, ga)

    (sm,) = all_reduce(1, [cross_gram(x.at[1, 2], x.at[1, 1])])
    gb = join(bs, sm, am)
    vb = whitening_t(gb)
    put(vb[bw:], x.at[1, 2], x.at[1, 1], into(x.at[2, 3]))
    bs, bm = new_grams(vb, gb)
    sent.append(pass_on(1, x.at[2, 3], bm))
    put(vb[:bw], x.at[1, 2], x.at[1, 1], into(x.at[2, 2]))
    put(va[:bw], x.at[0, 0], x.at[0, 1], into(x.at[1, 0]))

    for c in sent[0]:
        c.wait_recv()
    (sm,) = all_reduce(2, [cross_gram(x.at[1, 0], perm.at[0])])
    ga = join(as_, sm, gmm_in[0])
    va = whitening_t(ga)
    put(va[bw:], x.at[1, 0], perm.at[0], into(x.at[2, 1]))
    put(va[:bw], x.at[1, 0], perm.at[0], into(x.at[2, 0]))
    as_, am = new_grams(va, ga)

    sm_b = cross_gram(x.at[2, 2], x.at[2, 1])
    for c in sent[1]:
        c.wait_recv()
    sm_b, sm_a = all_reduce(3, [sm_b, cross_gram(x.at[2, 0], perm.at[1])])
    gb = join(bs, sm_b, am)
    vb = whitening_t(gb)
    put(vb[bw:], x.at[2, 2], x.at[2, 1], into(x.at[3, 3]))
    bs, bm = new_grams(vb, gb)
    sent.append(pass_on(2, x.at[3, 3], bm))
    ga = join(as_, sm_a, gmm_in[1])
    va = whitening_t(ga)
    put(va[bw:], x.at[2, 0], perm.at[1], into(x.at[3, 1]))
    put(vb[:bw], x.at[2, 2], x.at[2, 1], into(x.at[3, 2]))
    as_, am = new_grams(va, ga)

    (sm,) = all_reduce(4, [cross_gram(x.at[3, 2], x.at[3, 1])])
    gb = join(bs, sm, am)
    finish(1, whitening_t(gb), gb, x.at[3, 2], x.at[3, 1])
    put(va[:bw], x.at[2, 0], perm.at[1], into(x.at[3, 0]))
    for c in sent[2]:
        c.wait_recv()
    (sm,) = all_reduce(5, [cross_gram(x.at[3, 0], perm.at[2])])
    ga = join(as_, sm, gmm_in[2])
    finish(0, whitening_t(ga), ga, x.at[3, 0], perm.at[2])

    for b in range(len(COUNTS)):
        settle(b)
    for pair in sent:
        for c in pair:
            c.wait_send()
    pltpu.make_async_copy(send.at[0], out_ref.at[my_k], own_sem).wait()
    rest = send.at[pl.ds(0, n - 1)]
    pltpu.make_async_copy(rest, rest, out_s).wait()
    arrived = out_ref.at[pl.ds(0, n - 1)]
    pltpu.make_async_copy(arrived, arrived, out_r).wait()


COUNTS = (6, 1, 1, 2, 1, 1)


def on_device(observed, estimate, mask, threshold):
    n_rows = lax.axis_size("rows")
    n_pairs = lax.axis_size("pairs")
    rows, width = observed.shape
    bw = width // 4
    n = n_rows * n_pairs
    each = width // n
    step = 512 if rows % 512 == 0 else rows
    total = sum(COUNTS) * bw
    vmem = pl.BlockSpec(memory_space=pltpu.VMEM)
    dma = pltpu.SemaphoreType.DMA
    nb = len(COUNTS)
    landed = pl.pallas_call(
        functools.partial(kernel, n_rows, n_pairs, step),
        out_shape=jax.ShapeDtypeStruct((n, each, rows), F32),
        in_specs=[vmem] * 4,
        out_specs=pl.BlockSpec(memory_space=pl.ANY),
        scratch_shapes=[
            pltpu.VMEM((4, 4, bw, rows), F32),
            pltpu.VMEM((3, bw, rows), F32),
            pltpu.VMEM((total, bw), F32),
            pltpu.VMEM((n_rows, total // n_rows, bw), F32),
            pltpu.VMEM((total, bw), F32),
            pltpu.VMEM((3, bw, bw), F32),
            pltpu.VMEM((3, bw, bw), F32),
            pltpu.VMEM((8, bw), F32),
            pltpu.VMEM((n, each, rows), F32),
            dma((nb,)), dma((nb,)), dma((nb,)), dma((nb,)),
            dma((3,)), dma((3,)), dma((3,)), dma((3,)),
            dma, dma, dma,
        ],
        compiler_params=pltpu.CompilerParams(
            collective_id=0, has_side_effects=True, vmem_limit_bytes=60 * 1024 * 1024
        ),
    )(observed, estimate, mask, threshold.reshape(width, 1))
    landed = landed.reshape(n_rows, n_pairs, each, rows).transpose(2, 1, 0, 3)
    return landed.reshape(each * n_pairs, n_rows * rows)


def solution(mesh):
    placed = (P("rows", "pairs"), P("rows", "pairs"), P("rows", "pairs"), P("pairs"))
    return jax.shard_map(
        on_device, mesh=mesh, in_specs=placed, out_specs=P(("rows", "pairs"), None), check_vma=False
    )
```

```python
import functools

import jax
import jax.numpy as jnp
from jax import lax
from jax.experimental import pallas as pl
from jax.experimental.pallas import tpu as pltpu
from jax.sharding import PartitionSpec as P

MESH = pl.DeviceIdType.MESH
F32 = jnp.float32
BF16 = jnp.bfloat16
NN = (((1,), (0,)), ((), ()))
NT = (((1,), (1,)), ((), ()))


def split(a):
    high = a.astype(BF16)
    return high, (a - high.astype(F32)).astype(BF16)


def dot_parts(a, b, dims):
    def one(x, y):
        return lax.dot_general(x, y, dims, preferred_element_type=F32)

    return one(a[0], b[0]) + (one(a[0], b[1]) + one(a[1], b[0]))


def dot3(a, b, dims=NN):
    return dot_parts(split(a), split(b), dims)


def whitening_t(gram):
    width = gram.shape[0]
    eye = (
        lax.broadcasted_iota(jnp.int32, (width, width), 0)
        == lax.broadcasted_iota(jnp.int32, (width, width), 1)
    ).astype(F32)
    on_diag = gram * eye
    d_col = jnp.sum(on_diag, axis=1, keepdims=True) + 1e-06
    d_row = jnp.sum(on_diag, axis=0, keepdims=True) + 1e-06
    i_col = 1.0 / jnp.sqrt(d_col)
    i_row = 1.0 / jnp.sqrt(d_row)
    normed = gram * i_col * i_row
    sq = jnp.sum(jnp.sum(normed * normed, axis=1, keepdims=True), axis=0, keepdims=True)
    fro = jnp.sqrt(sq)
    y = normed / fro
    t = 1.5 * eye - 0.5 * y
    z = t
    y = dot3(y, t)
    t = 1.5 * eye - 0.5 * dot3(z, y)
    y, z = dot3(y, t), dot3(t, z)
    t = 1.5 * eye - 0.5 * dot3(z, y)
    z = dot3(t, z)
    return jnp.sqrt(d_col) * z * i_row / jnp.sqrt(fro)


def join(ss, sm, mm):
    top = jnp.concatenate([ss, sm], axis=1)
    low = jnp.concatenate([sm.T, mm], axis=1)
    return jnp.concatenate([top, low], axis=0)


def kernel(
    n_rows, n_pairs, step,
    obs_ref, est_ref, mask_ref, thr_ref, out_ref,
    x, perm, pay, land, res, gmm_out, gmm_in, send,
    rs_s, rs_r, ag_s, ag_r, pm_s, pm_r, pg_s, pg_r, out_s, out_r, own_sem,
):
    me = lax.axis_index("rows")
    group = lax.axis_index("pairs")
    n = n_rows * n_pairs
    bw = x.shape[2]
    rows = x.shape[3]
    chunks = rows // step
    each = send.shape[1]

    barrier = pltpu.get_barrier_semaphore()
    my_k = me * n_pairs + group

    def greet(i, carry):
        k = lax.rem(my_k + i, n)
        pl.semaphore_signal(
            barrier, inc=1, device_id=(k // n_pairs, lax.rem(k, n_pairs)), device_id_type=MESH
        )
        return carry

    lax.fori_loop(1, n, greet, 0)

    for slot in range(4):
        cols = slice(slot * bw, (slot + 1) * bw)
        for c in range(chunks):
            part = slice(c * step, (c + 1) * step)
            filled = jnp.where(mask_ref[part, cols] == 1, obs_ref[part, cols], est_ref[part, cols])
            x[0, slot, :, part] = filled.T

    def cols_of(c):
        return pl.ds(pl.multiple_of(c * step, step), step)

    def full_gram(s, m):
        total = jnp.zeros((2 * bw, 2 * bw), F32)
        for c in range(chunks):
            part = slice(c * step, (c + 1) * step)
            both = split(jnp.concatenate([s[:, part], m[:, part]], axis=0))
            total += dot_parts(both, both, NT)
        return total

    def cross_gram(s, m):
        total = jnp.zeros((bw, bw), F32)
        for c in range(chunks):
            part = slice(c * step, (c + 1) * step)
            total += dot_parts(split(s[:, part]), split(m[:, part]), NT)
        return total

    def all_reduce(b, blocks):
        count = len(blocks)
        piece = count * bw // n_rows
        base = sum(COUNTS[:b]) * bw
        lbase = base // n_rows
        for i, block in enumerate(blocks):
            pay[base + i * bw : base + (i + 1) * bw, :] = block
        if b == 0:
            pl.semaphore_wait(barrier, n - 1)

        def area(ref, p):
            return ref.at[pl.ds(pl.multiple_of(base + p * piece, 8), piece)]

        def scatter(off, carry):
            peer = lax.rem(me + off, n_rows)
            pltpu.make_async_remote_copy(
                area(pay, peer), land.at[off, pl.ds(lbase, piece)],
                rs_s.at[b], rs_r.at[b], device_id=(peer, group), device_id_type=MESH,
            ).start()
            return carry

        lax.fori_loop(1, n_rows, scatter, 0)
        others = land.at[pl.ds(1, n_rows - 1), pl.ds(lbase, piece)]
        pltpu.make_async_copy(others, others, rs_r.at[b]).wait()
        mine = pl.ds(pl.multiple_of(base + me * piece, 8), piece)
        total = pay[mine, :]
        for off in range(1, n_rows):
            total += land[off, lbase : lbase + piece, :]
        res[mine, :] = total

        def gather(off, carry):
            peer = lax.rem(me + off, n_rows)
            pltpu.make_async_remote_copy(
                area(res, me), area(res, me),
                ag_s.at[b], ag_r.at[b], device_id=(peer, group), device_id_type=MESH,
            ).start()
            return carry

        lax.fori_loop(1, n_rows, gather, 0)
        pltpu.make_async_copy(others, others, ag_r.at[b]).wait()
        return [res[base + i * bw : base + (i + 1) * bw, :] for i in range(count)]

    def settle(b):
        piece = COUNTS[b] * bw // n_rows
        lbase = sum(COUNTS[:b]) * bw // n_rows
        others = land.at[pl.ds(1, n_rows - 1), pl.ds(lbase, piece)]
        pltpu.make_async_copy(others, others, rs_s.at[b]).wait()
        pltpu.make_async_copy(others, others, ag_s.at[b]).wait()

    def put(v_half, s, m, write):
        v_parts = split(v_half)
        for c in range(chunks):
            part = slice(c * step, (c + 1) * step)
            both = split(jnp.concatenate([s[:, part], m[:, part]], axis=0))
            write(part, dot_parts(v_parts, both, NN))

    def into(ref):
        def write(part, value):
            ref[:, part] = value
        return write

    def pass_on(i, block, gmm):
        gmm_out[i] = gmm
        right = lax.rem(group + 1, n_pairs)
        data = pltpu.make_async_remote_copy(
            block, perm.at[i], pm_s.at[i], pm_r.at[i],
            device_id=(me, right), device_id_type=MESH,
        )
        data.start()
        small = pltpu.make_async_remote_copy(
            gmm_out.at[i], gmm_in.at[i], pg_s.at[i], pg_r.at[i],
            device_id=(me, right), device_id_type=MESH,
        )
        small.start()
        return data, small

    def new_grams(v, gram):
        vg = dot3(v, gram)
        return dot3(vg[:bw], v[:bw], NT), dot3(vg[bw:], v[bw:], NT)

    def deliver(half):
        count = n // 2

        def go(i, carry):
            k = half * count + lax.rem(my_k + i, count)

            @pl.when(k != my_k)
            def _():
                pltpu.make_async_remote_copy(
                    send.at[k], out_ref.at[my_k], out_s, out_r,
                    device_id=(k // n_pairs, lax.rem(k, n_pairs)), device_id_type=MESH,
                ).start()

            @pl.when(k == my_k)
            def _():
                pltpu.make_async_copy(send.at[k], out_ref.at[my_k], own_sem).start()

            return carry

        lax.fori_loop(0, count, go, 0)

    def finish(half, v, gram, s, m):
        vg = dot3(v, gram)
        squares = jnp.sum(vg * v, axis=1, keepdims=True)
        norm = jnp.sqrt(squares + 1e-06)
        eye = (
            lax.broadcasted_iota(jnp.int32, gram.shape, 0)
            == lax.broadcasted_iota(jnp.int32, gram.shape, 1)
        )
        level = thr_ref[:, 2 * half * bw : 2 * (half + 1) * bw]
        level = jnp.sum(jnp.where(eye, level, 0.0), axis=1, keepdims=True)
        scaled = (jnp.maximum(norm - level, 0.0) / norm) * v
        per_block = bw // each
        for j in range(2):
            def write(part, value):
                for i in range(per_block):
                    send[(2 * half + j) * per_block + i, :, part] = value[i * each : (i + 1) * each]
            put(scaled[j * bw : (j + 1) * bw], s, m, write)

    ga = full_gram(x.at[0, 0], x.at[0, 1])
    gb = full_gram(x.at[0, 2], x.at[0, 3])
    blocks = []
    for g in (ga, gb):
        blocks += [g[:bw, :bw], g[:bw, bw:], g[bw:, bw:]]
    got = all_reduce(0, blocks)
    gb = join(*got[3:])
    vb = whitening_t(gb)
    put(vb[bw:], x.at[0, 2], x.at[0, 3], into(x.at[1, 3]))
    bs, bm = new_grams(vb, gb)
    sent = [pass_on(0, x.at[1, 3], bm)]
    ga = join(*got[:3])
    va = whitening_t(ga)
    put(va[bw:], x.at[0, 0], x.at[0, 1], into(x.at[1, 1]))
    put(vb[:bw], x.at[0, 2], x.at[0, 3], into(x.at[1, 2]))
    as_, am = new_grams(va, ga)

    (sm,) = all_reduce(1, [cross_gram(x.at[1, 2], x.at[1, 1])])
    gb = join(bs, sm, am)
    vb = whitening_t(gb)
    put(vb[bw:], x.at[1, 2], x.at[1, 1], into(x.at[2, 3]))
    bs, bm = new_grams(vb, gb)
    sent.append(pass_on(1, x.at[2, 3], bm))
    put(vb[:bw], x.at[1, 2], x.at[1, 1], into(x.at[2, 2]))
    put(va[:bw], x.at[0, 0], x.at[0, 1], into(x.at[1, 0]))

    for c in sent[0]:
        c.wait_recv()
    (sm,) = all_reduce(2, [cross_gram(x.at[1, 0], perm.at[0])])
    ga = join(as_, sm, gmm_in[0])
    va = whitening_t(ga)
    put(va[bw:], x.at[1, 0], perm.at[0], into(x.at[2, 1]))
    put(va[:bw], x.at[1, 0], perm.at[0], into(x.at[2, 0]))
    as_, am = new_grams(va, ga)

    sm_b = cross_gram(x.at[2, 2], x.at[2, 1])
    for c in sent[1]:
        c.wait_recv()
    sm_b, sm_a = all_reduce(3, [sm_b, cross_gram(x.at[2, 0], perm.at[1])])
    gb = join(bs, sm_b, am)
    vb = whitening_t(gb)
    put(vb[bw:], x.at[2, 2], x.at[2, 1], into(x.at[3, 3]))
    bs, bm = new_grams(vb, gb)
    sent.append(pass_on(2, x.at[3, 3], bm))
    ga = join(as_, sm_a, gmm_in[1])
    va = whitening_t(ga)
    put(va[bw:], x.at[2, 0], perm.at[1], into(x.at[3, 1]))
    put(vb[:bw], x.at[2, 2], x.at[2, 1], into(x.at[3, 2]))
    as_, am = new_grams(va, ga)

    (sm,) = all_reduce(4, [cross_gram(x.at[3, 2], x.at[3, 1])])
    gb = join(bs, sm, am)
    finish(1, whitening_t(gb), gb, x.at[3, 2], x.at[3, 1])
    put(va[:bw], x.at[2, 0], perm.at[1], into(x.at[3, 0]))
    for c in sent[2]:
        c.wait_recv()
    (sm,) = all_reduce(5, [cross_gram(x.at[3, 0], perm.at[2])])
    ga = join(as_, sm, gmm_in[2])
    finish(0, whitening_t(ga), ga, x.at[3, 0], perm.at[2])
    far = 1 - my_k // (n // 2)
    deliver(far)
    deliver(1 - far)

    for b in range(len(COUNTS)):
        settle(b)
    for pair in sent:
        for c in pair:
            c.wait_send()
    pltpu.make_async_copy(send.at[0], out_ref.at[my_k], own_sem).wait()
    rest = send.at[pl.ds(0, n - 1)]
    pltpu.make_async_copy(rest, rest, out_s).wait()
    arrived = out_ref.at[pl.ds(0, n - 1)]
    pltpu.make_async_copy(arrived, arrived, out_r).wait()


def interleave(in_ref, out_ref):
    n_pairs, each, _ = in_ref.shape
    for i in range(each):
        out_ref[i * n_pairs : (i + 1) * n_pairs, :] = in_ref[:, i, :]


COUNTS = (6, 1, 1, 2, 1, 1)


def on_device(observed, estimate, mask, threshold):
    n_rows = lax.axis_size("rows")
    n_pairs = lax.axis_size("pairs")
    rows, width = observed.shape
    bw = width // 4
    n = n_rows * n_pairs
    each = width // n
    step = 512 if rows % 512 == 0 else rows
    total = sum(COUNTS) * bw
    vmem = pl.BlockSpec(memory_space=pltpu.VMEM)
    dma = pltpu.SemaphoreType.DMA
    nb = len(COUNTS)
    landed = pl.pallas_call(
        functools.partial(kernel, n_rows, n_pairs, step),
        out_shape=jax.ShapeDtypeStruct((n, each, rows), F32),
        in_specs=[vmem] * 4,
        out_specs=pl.BlockSpec(memory_space=pl.ANY),
        scratch_shapes=[
            pltpu.VMEM((4, 4, bw, rows), F32),
            pltpu.VMEM((3, bw, rows), F32),
            pltpu.VMEM((total, bw), F32),
            pltpu.VMEM((n_rows, total // n_rows, bw), F32),
            pltpu.VMEM((total, bw), F32),
            pltpu.VMEM((3, bw, bw), F32),
            pltpu.VMEM((3, bw, bw), F32),
            pltpu.VMEM((n, each, rows), F32),
            dma((nb,)), dma((nb,)), dma((nb,)), dma((nb,)),
            dma((3,)), dma((3,)), dma((3,)), dma((3,)),
            dma, dma, dma,
        ],
        compiler_params=pltpu.CompilerParams(
            collective_id=0, has_side_effects=True, vmem_limit_bytes=60 * 1024 * 1024
        ),
    )(observed, estimate, mask, threshold.reshape(1, width))
    landed = landed.reshape(n_rows, n_pairs, each, rows)
    return pl.pallas_call(
        interleave,
        grid=(n_rows,),
        out_shape=jax.ShapeDtypeStruct((each * n_pairs, n_rows * rows), F32),
        in_specs=[pl.BlockSpec((None, n_pairs, each, rows), lambda r: (r, 0, 0, 0))],
        out_specs=pl.BlockSpec((each * n_pairs, rows), lambda r: (0, r)),
    )(landed)


def solution(mesh):
    placed = (P("rows", "pairs"), P("rows", "pairs"), P("rows", "pairs"), P("pairs"))
    return jax.shard_map(
        on_device, mesh=mesh, in_specs=placed, out_specs=P(("rows", "pairs"), None), check_vma=False
    )
```

```python
import functools

import jax
import jax.numpy as jnp
from jax import lax
from jax.experimental import pallas as pl
from jax.experimental.pallas import tpu as pltpu
from jax.sharding import PartitionSpec as P

MESH = pl.DeviceIdType.MESH
F32 = jnp.float32
BF16 = jnp.bfloat16
NN = (((1,), (0,)), ((), ()))
NT = (((1,), (1,)), ((), ()))


def split(a):
    high = a.astype(BF16)
    return high, (a - high.astype(F32)).astype(BF16)


def dot_parts(a, b, dims):
    def one(x, y):
        return lax.dot_general(x, y, dims, preferred_element_type=F32)

    return one(a[0], b[0]) + (one(a[0], b[1]) + one(a[1], b[0]))


def dot3(a, b, dims=NN):
    return dot_parts(split(a), split(b), dims)


def whitening_t(gram):
    width = gram.shape[0]
    eye = (
        lax.broadcasted_iota(jnp.int32, (width, width), 0)
        == lax.broadcasted_iota(jnp.int32, (width, width), 1)
    ).astype(F32)
    on_diag = gram * eye
    d_col = jnp.sum(on_diag, axis=1, keepdims=True) + 1e-06
    d_row = jnp.sum(on_diag, axis=0, keepdims=True) + 1e-06
    i_col = 1.0 / jnp.sqrt(d_col)
    i_row = 1.0 / jnp.sqrt(d_row)
    normed = gram * i_col * i_row
    sq = jnp.sum(jnp.sum(normed * normed, axis=1, keepdims=True), axis=0, keepdims=True)
    fro = jnp.sqrt(sq)
    y = normed / fro
    t = 1.5 * eye - 0.5 * y
    z = t
    y = dot3(y, t)
    t = 1.5 * eye - 0.5 * dot3(z, y)
    y, z = dot3(y, t), dot3(t, z)
    t = 1.5 * eye - 0.5 * dot3(z, y)
    z = dot3(t, z)
    return jnp.sqrt(d_col) * z * i_row / jnp.sqrt(fro)


def join(ss, sm, mm):
    top = jnp.concatenate([ss, sm], axis=1)
    low = jnp.concatenate([sm.T, mm], axis=1)
    return jnp.concatenate([top, low], axis=0)


def kernel(
    n_rows, n_pairs, step,
    obs_ref, est_ref, mask_ref, thr_ref, out_ref,
    x, perm, pay, land, res, gmm_out, gmm_in, send,
    rs_s, rs_r, ag_s, ag_r, pm_s, pm_r, pg_s, pg_r, out_s, out_r, own_sem,
):
    me = lax.axis_index("rows")
    group = lax.axis_index("pairs")
    n = n_rows * n_pairs
    bw = x.shape[2]
    rows = x.shape[3]
    chunks = rows // step
    each = send.shape[1]

    barrier = pltpu.get_barrier_semaphore()
    my_k = me * n_pairs + group

    def greet(i, carry):
        k = lax.rem(my_k + i, n)
        pl.semaphore_signal(
            barrier, inc=1, device_id=(k // n_pairs, lax.rem(k, n_pairs)), device_id_type=MESH
        )
        return carry

    lax.fori_loop(1, n, greet, 0)

    for slot in range(4):
        cols = slice(slot * bw, (slot + 1) * bw)
        for c in range(chunks):
            part = slice(c * step, (c + 1) * step)
            filled = jnp.where(mask_ref[part, cols] == 1, obs_ref[part, cols], est_ref[part, cols])
            x[0, slot, :, part] = filled.T

    def cols_of(c):
        return pl.ds(pl.multiple_of(c * step, step), step)

    def full_gram(s, m):
        total = jnp.zeros((2 * bw, 2 * bw), F32)
        for c in range(chunks):
            part = slice(c * step, (c + 1) * step)
            both = split(jnp.concatenate([s[:, part], m[:, part]], axis=0))
            total += dot_parts(both, both, NT)
        return total

    def cross_gram(s, m):
        total = jnp.zeros((bw, bw), F32)
        for c in range(chunks):
            part = slice(c * step, (c + 1) * step)
            total += dot_parts(split(s[:, part]), split(m[:, part]), NT)
        return total

    def place(b):
        base = sum(COUNTS[:b]) * bw
        piece = COUNTS[b] * bw // n_rows
        return base, base // n_rows, piece

    def own(b, p):
        base, _, piece = place(b)
        return pl.ds(pl.multiple_of(base + p * piece, 8), piece)

    def others(b):
        _, lbase, piece = place(b)
        return land.at[pl.ds(1, n_rows - 1), pl.ds(lbase, piece)]

    def reduce_start(b, blocks):
        base, lbase, piece = place(b)
        for i, block in enumerate(blocks):
            pay[base + i * bw : base + (i + 1) * bw, :] = block
        if b == 0:
            pl.semaphore_wait(barrier, n - 1)

        def scatter(off, carry):
            peer = lax.rem(me + off, n_rows)
            pltpu.make_async_remote_copy(
                pay.at[own(b, peer)], land.at[off, pl.ds(lbase, piece)],
                rs_s.at[b], rs_r.at[b], device_id=(peer, group), device_id_type=MESH,
            ).start()
            return carry

        lax.fori_loop(1, n_rows, scatter, 0)

    def reduce_mid(b):
        _, lbase, piece = place(b)
        pltpu.make_async_copy(others(b), others(b), rs_r.at[b]).wait()
        mine = own(b, me)
        total = pay[mine, :]
        for off in range(1, n_rows):
            total += land[off, lbase : lbase + piece, :]
        res[mine, :] = total

        def gather(off, carry):
            peer = lax.rem(me + off, n_rows)
            pltpu.make_async_remote_copy(
                res.at[mine], res.at[mine],
                ag_s.at[b], ag_r.at[b], device_id=(peer, group), device_id_type=MESH,
            ).start()
            return carry

        lax.fori_loop(1, n_rows, gather, 0)

    def reduce_end(b):
        base, _, _ = place(b)
        pltpu.make_async_copy(others(b), others(b), ag_r.at[b]).wait()
        return [res[base + i * bw : base + (i + 1) * bw, :] for i in range(COUNTS[b])]

    def settle(b):
        pltpu.make_async_copy(others(b), others(b), rs_s.at[b]).wait()
        pltpu.make_async_copy(others(b), others(b), ag_s.at[b]).wait()

    def put(v_half, s, m, write):
        v_parts = split(v_half)
        for c in range(chunks):
            part = slice(c * step, (c + 1) * step)
            both = split(jnp.concatenate([s[:, part], m[:, part]], axis=0))
            write(part, dot_parts(v_parts, both, NN))

    def into(ref):
        def write(part, value):
            ref[:, part] = value
        return write

    right = lax.rem(group + 1, n_pairs)

    def pass_copy(src, dst, send_sem, recv_sem):
        return pltpu.make_async_remote_copy(
            src, dst, send_sem, recv_sem, device_id=(me, right), device_id_type=MESH
        )

    def put_and_pass(i, v_half, s, m, block):
        def write(part, value):
            block[:, part] = value
            pass_copy(block.at[:, part], perm.at[i, :, part], pm_s.at[i], pm_r.at[i]).start()

        put(v_half, s, m, write)

    def pass_gram(i, block, gmm):
        gmm_out[i] = gmm
        small = pass_copy(gmm_out.at[i], gmm_in.at[i], pg_s.at[i], pg_r.at[i])
        small.start()
        return pass_copy(block, perm.at[i], pm_s.at[i], pm_r.at[i]), small

    def new_grams(v, gram):
        vg = dot3(v, gram)
        return dot3(vg[:bw], v[:bw], NT), dot3(vg[bw:], v[bw:], NT)

    def deliver(half):
        count = n // 2

        def go(i, carry):
            k = half * count + lax.rem(my_k + i, count)

            @pl.when(k != my_k)
            def _():
                pltpu.make_async_remote_copy(
                    send.at[k], out_ref.at[my_k], out_s, out_r,
                    device_id=(k // n_pairs, lax.rem(k, n_pairs)), device_id_type=MESH,
                ).start()

            @pl.when(k == my_k)
            def _():
                pltpu.make_async_copy(send.at[k], out_ref.at[my_k], own_sem).start()

            return carry

        lax.fori_loop(0, count, go, 0)

    def finish(half, v, gram, s, m):
        vg = dot3(v, gram)
        squares = jnp.sum(vg * v, axis=1, keepdims=True)
        norm = jnp.sqrt(squares + 1e-06)
        eye = (
            lax.broadcasted_iota(jnp.int32, gram.shape, 0)
            == lax.broadcasted_iota(jnp.int32, gram.shape, 1)
        )
        level = thr_ref[:, 2 * half * bw : 2 * (half + 1) * bw]
        level = jnp.sum(jnp.where(eye, level, 0.0), axis=1, keepdims=True)
        scaled = (jnp.maximum(norm - level, 0.0) / norm) * v
        per_block = bw // each
        for j in range(2):
            def write(part, value):
                for i in range(per_block):
                    send[(2 * half + j) * per_block + i, :, part] = value[i * each : (i + 1) * each]
            put(scaled[j * bw : (j + 1) * bw], s, m, write)

    def thirds(g):
        return [g[:bw, :bw], g[:bw, bw:], g[bw:, bw:]]

    reduce_start(0, thirds(full_gram(x.at[0, 2], x.at[0, 3])))
    reduce_start(1, thirds(full_gram(x.at[0, 0], x.at[0, 1])))
    reduce_mid(0)
    reduce_mid(1)
    gb = join(*reduce_end(0))
    vb = whitening_t(gb)
    put_and_pass(0, vb[bw:], x.at[0, 2], x.at[0, 3], x.at[1, 3])
    bs, bm = new_grams(vb, gb)
    sent = [pass_gram(0, x.at[1, 3], bm)]
    put(vb[:bw], x.at[0, 2], x.at[0, 3], into(x.at[1, 2]))
    ga = join(*reduce_end(1))
    va = whitening_t(ga)
    put(va[bw:], x.at[0, 0], x.at[0, 1], into(x.at[1, 1]))

    reduce_start(2, [cross_gram(x.at[1, 2], x.at[1, 1])])
    put(va[:bw], x.at[0, 0], x.at[0, 1], into(x.at[1, 0]))
    reduce_mid(2)
    as_, am = new_grams(va, ga)
    gb = join(bs, *reduce_end(2), am)
    vb = whitening_t(gb)
    put_and_pass(1, vb[bw:], x.at[1, 2], x.at[1, 1], x.at[2, 3])
    bs, bm = new_grams(vb, gb)
    sent.append(pass_gram(1, x.at[2, 3], bm))

    for c in sent[0]:
        c.wait_recv()
    reduce_start(3, [cross_gram(x.at[1, 0], perm.at[0])])
    put(vb[:bw], x.at[1, 2], x.at[1, 1], into(x.at[2, 2]))
    reduce_mid(3)
    ga = join(as_, *reduce_end(3), gmm_in[0])
    va = whitening_t(ga)
    put(va[bw:], x.at[1, 0], perm.at[0], into(x.at[2, 1]))

    reduce_start(4, [cross_gram(x.at[2, 2], x.at[2, 1])])
    put(va[:bw], x.at[1, 0], perm.at[0], into(x.at[2, 0]))
    as_, am = new_grams(va, ga)
    for c in sent[1]:
        c.wait_recv()
    reduce_mid(4)
    reduce_start(5, [cross_gram(x.at[2, 0], perm.at[1])])
    gb = join(bs, *reduce_end(4), am)
    reduce_mid(5)
    vb = whitening_t(gb)
    put_and_pass(2, vb[bw:], x.at[2, 2], x.at[2, 1], x.at[3, 3])
    bs, bm = new_grams(vb, gb)
    sent.append(pass_gram(2, x.at[3, 3], bm))
    put(vb[:bw], x.at[2, 2], x.at[2, 1], into(x.at[3, 2]))
    ga = join(as_, *reduce_end(5), gmm_in[1])
    va = whitening_t(ga)
    put(va[bw:], x.at[2, 0], perm.at[1], into(x.at[3, 1]))

    reduce_start(6, [cross_gram(x.at[3, 2], x.at[3, 1])])
    put(va[:bw], x.at[2, 0], perm.at[1], into(x.at[3, 0]))
    as_, am = new_grams(va, ga)
    reduce_mid(6)
    gb = join(bs, *reduce_end(6), am)
    vb = whitening_t(gb)
    for c in sent[2]:
        c.wait_recv()
    reduce_start(7, [cross_gram(x.at[3, 0], perm.at[2])])
    finish(1, vb, gb, x.at[3, 2], x.at[3, 1])
    reduce_mid(7)
    ga = join(as_, *reduce_end(7), gmm_in[2])
    deliver(1)
    finish(0, whitening_t(ga), ga, x.at[3, 0], perm.at[2])
    deliver(0)

    for b in range(len(COUNTS)):
        settle(b)
    for pair in sent:
        for c in pair:
            c.wait_send()
    pltpu.make_async_copy(send.at[0], out_ref.at[my_k], own_sem).wait()
    rest = send.at[pl.ds(0, n - 1)]
    pltpu.make_async_copy(rest, rest, out_s).wait()
    arrived = out_ref.at[pl.ds(0, n - 1)]
    pltpu.make_async_copy(arrived, arrived, out_r).wait()


def interleave(in_ref, out_ref):
    n_pairs, each, _ = in_ref.shape
    for i in range(each):
        out_ref[i * n_pairs : (i + 1) * n_pairs, :] = in_ref[:, i, :]


COUNTS = (3, 3, 1, 1, 1, 1, 1, 1)


def on_device(observed, estimate, mask, threshold):
    n_rows = lax.axis_size("rows")
    n_pairs = lax.axis_size("pairs")
    rows, width = observed.shape
    bw = width // 4
    n = n_rows * n_pairs
    each = width // n
    step = 512 if rows % 512 == 0 else rows
    total = sum(COUNTS) * bw
    vmem = pl.BlockSpec(memory_space=pltpu.VMEM)
    dma = pltpu.SemaphoreType.DMA
    nb = len(COUNTS)
    landed = pl.pallas_call(
        functools.partial(kernel, n_rows, n_pairs, step),
        out_shape=jax.ShapeDtypeStruct((n, each, rows), F32),
        in_specs=[vmem] * 4,
        out_specs=pl.BlockSpec(memory_space=pl.ANY),
        scratch_shapes=[
            pltpu.VMEM((4, 4, bw, rows), F32),
            pltpu.VMEM((3, bw, rows), F32),
            pltpu.VMEM((total, bw), F32),
            pltpu.VMEM((n_rows, total // n_rows, bw), F32),
            pltpu.VMEM((total, bw), F32),
            pltpu.VMEM((3, bw, bw), F32),
            pltpu.VMEM((3, bw, bw), F32),
            pltpu.VMEM((n, each, rows), F32),
            dma((nb,)), dma((nb,)), dma((nb,)), dma((nb,)),
            dma((3,)), dma((3,)), dma((3,)), dma((3,)),
            dma, dma, dma,
        ],
        compiler_params=pltpu.CompilerParams(
            collective_id=0, has_side_effects=True, vmem_limit_bytes=60 * 1024 * 1024
        ),
    )(observed, estimate, mask, threshold.reshape(1, width))
    landed = landed.reshape(n_rows, n_pairs, each, rows)
    return pl.pallas_call(
        interleave,
        grid=(n_rows,),
        out_shape=jax.ShapeDtypeStruct((each * n_pairs, n_rows * rows), F32),
        in_specs=[pl.BlockSpec((None, n_pairs, each, rows), lambda r: (r, 0, 0, 0))],
        out_specs=pl.BlockSpec((each * n_pairs, rows), lambda r: (0, r)),
    )(landed)


def solution(mesh):
    placed = (P("rows", "pairs"), P("rows", "pairs"), P("rows", "pairs"), P("pairs"))
    return jax.shard_map(
        on_device, mesh=mesh, in_specs=placed, out_specs=P(("rows", "pairs"), None), check_vma=False
    )
```
